128 devices in a mesh: tm: 32 (over x, z, core), tp: 4 (over y).
Axes of the slice: x: 4, y: 4, z: 4, core: 2. Of those that a mesh axis runs over, the one named last changes fastest.
Arguments:
- trajectory: float32 [64, 128, 3072], P('tm', None, 'tp'), may hold values from -6 to 6
- offset: int32 [1], replicated, may hold values from 0 to 63
- step_gaps: int32 [64], P('tm'), may hold values from 1 to 4, as said below
- qkv_weight: bfloat16 [3072, 3, 3072], P(None, None, 'tp')
- out_weight: bfloat16 [3072, 3072], P('tp'), may hold values from -4 to 4
- mod_weight: bfloat16 [256, 3, 3072], P(None, None, 'tp'), may hold values from -0.375 to 0.375
Outputs:
- advanced: float32 [64, 128, 3072], P('tm', None, 'tp')
The draws below stay inside these ranges and needn't reach their ends.
Inputs may be any that keep to these rules, and one draw needn't show every extreme that they name: `step_gaps`: in aligned blocks of 2 timesteps, the gaps of block b sum to an even number for even b and to an odd number for odd b.
All inputs are finite; a program needn't handle non-finite values.
Results may differ from the reference program's by a relative error of at most 0.007.
Values may be sent and summed in bfloat16 or wider, within the bound.
No kernel may reach another device: no remote copies, remote signals or barrier semaphores. Data moves between devices by JAX's collectives and lax.ppermute only.
A program may use at most 128 MiB of HBM per device.

```python
import math
import jax
import jax.numpy as jnp
from jax import lax

D = 3072
HEADS = 24
HD = 128
FREQ = 256
TOK = 128
STEP_DEV = 2
ITERS = 2
TIME = 64
SCHED = 320


def draw_step_gaps(key, part):
    key_gaps = jax.random.fold_in(key, 37)
    gaps = jax.random.randint(key_gaps, (TIME,), 1, 5, dtype=jnp.int32)
    blocks = gaps.reshape(TIME // STEP_DEV, STEP_DEV)
    totals = jnp.sum(blocks, 1)
    parity = jnp.arange(TIME // STEP_DEV, dtype=jnp.int32) % 2
    wrong = totals % 2 != parity
    last_gap = blocks[:, -1]
    fixed_gap = jnp.where(last_gap < 4, last_gap + 1, 3)
    new_last = jnp.where(wrong, fixed_gap, last_gap)
    blocks = jnp.concatenate([blocks[:, :-1], new_last[:, None]], 1)
    return blocks.reshape(TIME).astype(jnp.int32)


def draw_qkv_weight(key, part):
    key_norm = jax.random.fold_in(key, 11)
    drawn = jax.random.normal(key_norm, (D, 3, D), jnp.float32) / math.sqrt(D)
    return drawn.astype(jnp.bfloat16)


def block_scale(stream_key, shape, cuts, low, top_value):
    factor_of, own = 1.0, jax.random.fold_in(stream_key, 6)
    for position, shards_of in cuts:
        steps = jnp.exp(jax.random.uniform(jax.random.fold_in(own, position), (shards_of,), jnp.float32, low / len(cuts), top_value / len(cuts)))
        factor_of = factor_of * jnp.repeat(steps, shape[position] // shards_of).reshape([-1 if axis == position else 1 for axis in range(len(shape))])
    return factor_of


def centred(rng, dims, scale, limit, cuts=(), kind=jnp.bfloat16):
    level = block_scale(rng, dims, cuts, -0.22, 0.18) if cuts else 1.0
    result = jax.random.normal(rng, dims, jnp.float32) * scale * level
    return jnp.minimum(jnp.maximum(result, -limit), limit).astype(kind)


def setup_inputs(seed: int = 0) -> dict:
    seeds = jax.random.split(jax.random.key(seed), 7)
    return {
        "trajectory": centred(seeds[0], (TIME, TOK, D), 1.0, 6.0, ((0, 32), (2, 4)), jnp.float32),
        "offset": jax.random.randint(seeds[1], (1,), 0, TIME).astype(jnp.int32),
        "step_gaps": draw_step_gaps(jax.random.fold_in(seeds[6], 71), 0),
        "qkv_weight": draw_qkv_weight(jax.random.fold_in(seeds[6], 71), 0),
        "out_weight": centred(seeds[4], (D, D), 0.25, 4.0, ((0, 4),)),
        "mod_weight": centred(seeds[5], (FREQ, 3, D), FREQ ** -0.5, 0.375, ((2, 4),)),
    }


def noise_levels(offset, step_gaps):
    before = jnp.cumsum(step_gaps) - step_gaps
    levels = (offset[0] + before).astype(jnp.float32)
    sigma = 1.0 - levels / SCHED
    step_size = step_gaps.astype(jnp.float32) / SCHED
    return (sigma, step_size)

def embedding(sigma):
    half_freq = FREQ // 2
    frequencies = jnp.exp(-math.log(10000.0) * jnp.arange(half_freq, dtype=jnp.float32) / half_freq)
    angles = 1000.0 * sigma[:, None] * frequencies[None, :]
    return jnp.concatenate([jnp.cos(angles), jnp.sin(angles)], -1).astype(jnp.bfloat16)

def one_head(triple):
    queries, key_rows, values = triple
    scores = jnp.dot(queries, key_rows.T, preferred_element_type=jnp.float32) * (1.0 / math.sqrt(HD))
    row_max = lax.optimization_barrier(jnp.max(scores, -1, keepdims=True))
    weights_exp = jnp.exp(scores - row_max)
    probs = (weights_exp / lax.optimization_barrier(jnp.sum(weights_exp, -1, keepdims=True))).astype(jnp.bfloat16)
    return jnp.dot(probs, values, preferred_element_type=jnp.float32).astype(jnp.bfloat16)

def drift_of(state, modulation, qkv_weight, out_weight):
    row_total = lax.optimization_barrier(jnp.sum(state, -1, keepdims=True))
    row_squares = lax.optimization_barrier(jnp.sum(state * state, -1, keepdims=True))
    row_mean = row_total / D
    variance = row_squares / D - row_mean * row_mean
    inv_std = lax.rsqrt(variance + 1e-06)
    normed = ((state - row_mean) * inv_std * (1.0 + modulation[1]) + modulation[0]).astype(jnp.bfloat16)
    projected = jnp.dot(normed, qkv_weight.reshape(D, 3 * D), preferred_element_type=jnp.float32)
    projected = projected.astype(jnp.bfloat16).reshape(TOK, 3, HEADS, HD)
    per_head = jnp.transpose(projected, (1, 2, 0, 3))
    attended = lax.map(one_head, (per_head[0], per_head[1], per_head[2]))
    attended = jnp.transpose(attended, (1, 0, 2)).reshape(TOK, D)
    head_out = jnp.dot(attended, out_weight, preferred_element_type=jnp.float32)
    return modulation[2] * head_out

def reference(trajectory, offset, step_gaps, qkv_weight, out_weight, mod_weight):
    sigma, step_size = noise_levels(offset, step_gaps)
    embed_rows = embedding(sigma)
    modulation = jnp.dot(embed_rows, mod_weight.reshape(FREQ, 3 * D), preferred_element_type=jnp.float32).reshape(TIME, 3, D)
    start_point = trajectory[0]
    states = trajectory
    points = trajectory
    for sweep in range(ITERS):
        drifts = lax.map(lambda pair: drift_of(pair[0], pair[1], qkv_weight, out_weight), (states, modulation))
        increments = -step_size[:, None, None] * drifts
        points = start_point[None] + jnp.cumsum(increments, 0)
        states = jnp.concatenate([start_point[None], points[:-1]], 0)
    return points
```

```python
import math

import jax
import jax.numpy as jnp
from jax import lax
from jax.experimental import pallas as pl
from jax.experimental.pallas import tpu as pltpu
from jax.sharding import PartitionSpec as P

HD = 128
FREQ = 256
ITERS = 2
NX, NZ, NC, NY = 4, 4, 2, 4
BF = jnp.bfloat16
F32 = jnp.float32


def ring(k):
    return [(i, (i + k) % NY) for i in range(NY)]


def place(x, z, c):
    return (x * NZ + z) * NC + c


CHIPS = [(x, z, c) for x in range(NX) for z in range(NZ) for c in range(NC)]
SWAP = [(place(x, z, c), place(x, z, 1 - c)) for x, z, c in CHIPS]


def z_shift(k):
    return [(place(x, z, c), place(x, (z + k) % NZ, c)) for x, z, c in CHIPS]


def x_shift(k):
    return [(place(x, z, c), place((x + k) % NX, z, c)) for x, z, c in CHIPS]


def spread(array):
    return [array] + [lax.ppermute(array, "tp", ring(k)) for k in (1, 2, 3)]


def deliver(own, blocks):
    total = own
    for k, block in zip((1, 2, 3), blocks, strict=True):
        total = total + lax.ppermute(block, "tp", ring(k)).astype(F32)
    return total


def embedding(sigma):
    half_freq = FREQ // 2
    frequencies = jnp.exp(-math.log(10000.0) * jnp.arange(half_freq, dtype=F32) / half_freq)
    angles = 1000.0 * sigma[:, None] * frequencies[None, :]
    return jnp.concatenate([jnp.cos(angles), jnp.sin(angles)], -1).astype(BF)


def block_body(first, tok, cols, me_ref, neg_ref, *refs):
    if first:
        states, refs = refs[:4], refs[4:]
        incs = means = None
    else:
        states, incs, means, refs = refs[:4], refs[4:8], refs[8:12], refs[12:]
    mods, (qkv_hbm, out_hbm), refs = refs[:4], refs[4:6], refs[6:]
    tots, ins, refs = refs[:4], refs[4:8], refs[8:]
    wv, wo, nrm, qkv, att, sems = refs
    me = me_ref[0]
    copies = []
    for p in range(3):
        for k in range(NY):
            src = lax.rem(me + NY - k, NY) * cols
            copies.append(
                pltpu.make_async_copy(
                    qkv_hbm.at[p, pl.ds(src, cols), :], wv.at[p, pl.ds(k * cols, cols), :], sems.at[p * NY + k]
                )
            )
    for k in range(NY):
        dst = lax.rem(me + k, NY) * cols
        copies.append(pltpu.make_async_copy(out_hbm.at[:, pl.ds(dst, cols)], wo.at[k], sems.at[3 * NY + k]))
    for copy in copies:
        copy.start()
    width = NY * cols
    for s in range(2):
        rows = pl.ds(s * tok, tok)
        parts = []
        for k in range(NY):
            if first:
                centre = jnp.transpose(mods[k][:, s * tok : (s + 1) * tok])[:, 6:7]
                x = states[k][rows, :].astype(F32) + centre
            else:
                centre = jnp.transpose(means[k][...])[:, 0:1]
                x = states[k][...].astype(F32) + centre
                if s == 1:
                    x = x + incs[k][...].astype(F32)
            parts.append(x)
        mean = sum(jnp.sum(x, -1, keepdims=True) for x in parts) / width
        var = sum(jnp.sum((x - mean) * (x - mean), -1, keepdims=True) for x in parts) / width
        inv = lax.rsqrt(var + 1e-06)
        for k in range(NY):
            shift = mods[k][3 * s : 3 * s + 1, :]
            scale = mods[k][3 * s + 1 : 3 * s + 2, :]
            normed = (parts[k] - mean) * inv * (1.0 + scale) + shift
            nrm[rows, k * cols : (k + 1) * cols] = normed.astype(BF)
    for p in range(3):
        for k in range(NY):
            copies[p * NY + k].wait()
        qkv[p] = jnp.dot(nrm[...], wv[p], preferred_element_type=F32).astype(BF)
    for s in range(2):
        rows = pl.ds(s * tok, tok)
        for h in range(cols // HD):
            lanes = pl.ds(h * HD, HD)
            scores = lax.dot_general(
                qkv[0, rows, lanes], qkv[1, rows, lanes], (((1,), (1,)), ((), ())), preferred_element_type=F32
            ) * (1.0 / math.sqrt(HD))
            weights = jnp.exp(scores - jnp.max(scores, -1, keepdims=True))
            probs = (weights * (1.0 / jnp.sum(weights, -1, keepdims=True))).astype(BF)
            att[rows, lanes] = jnp.dot(probs, qkv[2, rows, lanes], preferred_element_type=F32).astype(BF)
    for k in (1, 2, 3, 0):
        copies[3 * NY + k].wait()
        made = jnp.dot(att[...], wo[k], preferred_element_type=F32)
        gates = mods[(NY - k) % NY]
        inc0 = made[:tok] * (gates[2:3, :] * neg_ref[0])
        inc1 = made[tok:] * (gates[5:6, :] * neg_ref[1])
        tots[k][...] = (inc0 + inc1).astype(tots[k].dtype)
        ins[k][...] = inc0.astype(ins[k].dtype)


def block(first, me, neg, states, mods, qkv_weight, out_weight):
    cols, width = out_weight.shape
    tok = states[0].shape[0] // (2 if first else 1)
    n_arrays = len(states)
    outs = [jax.ShapeDtypeStruct((tok, cols), F32 if k == 0 else BF) for k in range(NY)]

    def body(*refs):
        block_body(first, tok, cols, *refs)

    vmem = pl.BlockSpec(memory_space=pltpu.VMEM)
    smem = pl.BlockSpec(memory_space=pltpu.SMEM)
    hbm = pl.BlockSpec(memory_space=pl.ANY)
    made = pl.pallas_call(
        body,
        out_shape=outs + outs,
        in_specs=[smem, smem] + [vmem] * (n_arrays + NY) + [hbm, hbm],
        out_specs=[vmem] * (2 * NY),
        scratch_shapes=[
            pltpu.VMEM((3, width, cols), BF),
            pltpu.VMEM((NY, cols, cols), BF),
            pltpu.VMEM((2 * tok, width), BF),
            pltpu.VMEM((3, 2 * tok, cols), BF),
            pltpu.VMEM((2 * tok, cols), BF),
            pltpu.SemaphoreType.DMA((4 * NY,)),
        ],
        compiler_params=pltpu.CompilerParams(vmem_limit_bytes=48 * 2**20),
        cost_estimate=pl.CostEstimate(
            flops=2 * 2 * tok * width * 4 * cols, bytes_accessed=8 * width * cols, transcendentals=0
        ),
        name="block",
    )(me, neg, *states, *mods, qkv_weight, out_weight)
    return made[:NY], made[NY:]


def body(trajectory, offset, step_gaps, qkv_weight, out_weight, mod_weight):
    steps_here, tok, cols = trajectory.shape
    width = qkv_weight.shape[0]
    tm, tp = lax.axis_index("tm"), lax.axis_index("tp")
    x_at, z_at, core = tm // (NZ * NC), (tm // NC) % NZ, tm % NC
    time_count = steps_here * lax.axis_size("tm")
    level_count = 5 * time_count
    half = tok // 2

    means = jnp.sum(trajectory, -1) / cols
    centred = (trajectory - means[:, :, None]).astype(BF).reshape(steps_here * tok, cols)
    first_states = spread(centred)

    gap_sum = jnp.sum(step_gaps)
    all_gaps = lax.all_to_all(jnp.broadcast_to(gap_sum, (NX * NZ * NC, 1, 128)), "tm", 0, 0)[:, 0, 0]
    before = jnp.sum(jnp.where(jnp.arange(NX * NZ * NC) < tm, all_gaps, 0))
    gap0, gap1 = step_gaps[0], step_gaps[1]
    levels = (offset[0] + before + jnp.stack([jnp.zeros_like(gap0), gap0])).astype(F32)
    sigma = 1.0 - levels / level_count
    step_size = jnp.stack([gap0, gap1]).astype(F32) / level_count
    flat_mod = jnp.transpose(mod_weight, (1, 0, 2))
    modulation = jnp.stack(
        [jnp.dot(embedding(sigma), flat_mod[p], preferred_element_type=F32) for p in range(3)], 1
    ).reshape(6, cols)
    mean_row = jnp.pad(means.reshape(1, steps_here * tok), ((0, 1), (0, cols - steps_here * tok)))
    mods = spread(jnp.concatenate([modulation, mean_row], 0))

    base = jnp.where(tm == 0, trajectory[0], 0.0)
    for pairs in (
        [(place(0, 0, 0), place(1, 0, 0))],
        [(place(0, 0, 0), place(3, 0, 0)), (place(1, 0, 0), place(2, 0, 0))],
        [(place(x, 0, 0), place(x, 1, 0)) for x in range(NX)],
        [(place(x, a, 0), place(x, b, 0)) for x in range(NX) for a, b in ((0, 3), (1, 2))],
        [(place(x, z, 0), place(x, z, 1)) for x in range(NX) for z in range(NZ)],
    ):
        base = base + lax.ppermute(base, "tm", pairs)
    base_mean = jnp.sum(base, -1) / cols
    base_means = spread(jnp.broadcast_to(base_mean[None], (8, tok)))

    me = jnp.reshape(tp, (1,)).astype(jnp.int32)
    neg = -step_size
    weights = (jnp.transpose(qkv_weight, (1, 0, 2)), out_weight)

    def scan(total):
        sent = total.astype(BF)
        other = lax.ppermute(sent, "tm", SWAP).astype(F32)
        chip = sent.astype(F32) + other
        mine = jnp.where(core == 0, chip[:half], chip[half:]).astype(BF)
        plane = mine.astype(F32)
        below = jnp.zeros_like(plane)
        for k in (1, 2, 3):
            came = lax.ppermute(mine, "tm", z_shift(k)).astype(F32)
            plane = plane + came
            below = below + jnp.where(z_at >= k, came, 0.0)
        plane = plane.astype(BF)
        for k in (1, 2, 3):
            came = lax.ppermute(plane, "tm", x_shift(k)).astype(F32)
            below = below + jnp.where(x_at >= k, came, 0.0)
        below = below.astype(BF)
        rest = lax.ppermute(below, "tm", SWAP)
        low = jnp.where(core == 0, below, rest)
        high = jnp.where(core == 0, rest, below)
        prefix = jnp.concatenate([low, high], 0).astype(F32)
        return base + prefix + jnp.where(core == 0, 0.0, other)

    states = first_states
    for sweep in range(ITERS):
        tots, incs = block(sweep == 0, me, neg, states, mods, *weights)
        total = deliver(tots[0], tots[1:])
        inc0 = deliver(incs[0], incs[1:])
        entry = scan(total)
        if sweep + 1 < ITERS:
            states = (
                spread((entry - base_mean[:, None]).astype(BF)) + spread(inc0.astype(BF)) + base_means
            )
    return jnp.stack([entry + inc0, entry + total])


def solution(mesh):
    placed = (
        P("tm", None, "tp"),
        P(),
        P("tm"),
        P(None, None, "tp"),
        P("tp", None),
        P(None, None, "tp"),
    )
    return jax.shard_map(
        body, mesh=mesh, in_specs=placed, out_specs=P("tm", None, "tp"), check_vma=False
    )
```

```python
import math

import jax
import jax.numpy as jnp
from jax import lax
from jax.experimental import pallas as pl
from jax.experimental.pallas import tpu as pltpu
from jax.sharding import PartitionSpec as P

HD = 128
FREQ = 256
EXTRA = 8
LIMIT = 48
CUTS = 1
LEVELS = 320
NX, NZ, NC, NY = 4, 4, 2, 4
BF = jnp.bfloat16
F32 = jnp.float32


def ring(k):
    return [(i, (i + k) % NY) for i in range(NY)]


def place(x, z, c):
    return (x * NZ + z) * NC + c


CHIPS = [(x, z, c) for x in range(NX) for z in range(NZ) for c in range(NC)]
SWAP = [(place(x, z, c), place(x, z, 1 - c)) for x, z, c in CHIPS]


def z_shift(k):
    return [(place(x, z, c), place(x, (z + k) % NZ, c)) for x, z, c in CHIPS]


def x_shift(k):
    return [(place(x, z, c), place((x + k) % NX, z, c)) for x, z, c in CHIPS]


def spread(array):
    return [array] + [lax.ppermute(array, "tp", ring(k)) for k in (1, 2, 3)]


def modulation_body(facts, all_gaps, mod_ref, out_ref):
    half_freq = FREQ // 2
    gaps = all_gaps[...]
    earlier = lax.broadcasted_iota(jnp.int32, gaps.shape, 0) < facts[0]
    before = jnp.sum(jnp.where(earlier, gaps, 0), 0)
    level = before[:, 0:1] + before[:, 1:2] + facts[2]
    lane = lax.broadcasted_iota(jnp.int32, (1, half_freq), 1).astype(F32)
    frequencies = jnp.exp(-math.log(10000.0) * lane / half_freq)
    rows = []
    for here in (level, level + facts[3]):
        angles = 1000.0 * (1.0 - here.astype(F32) / LEVELS) * frequencies
        rows.append(jnp.concatenate([jnp.cos(angles), jnp.sin(angles)], -1))
    index = lax.broadcasted_iota(jnp.int32, (8, FREQ), 0)
    embed_rows = jnp.where(index == 0, rows[0], jnp.where(index == 1, rows[1], 0.0)).astype(BF)
    out_ref[...] = jnp.zeros_like(out_ref)
    for p in range(3):
        made = jnp.dot(embed_rows, mod_ref[p], preferred_element_type=F32)
        for s in range(2):
            for y in range(NY):
                out_ref[y, 3 * s + p : 3 * s + p + 1, :] = made[s : s + 1]


def modulation(facts, all_gaps, mod_weight):
    vmem = pl.BlockSpec(memory_space=pltpu.VMEM)
    smem = pl.BlockSpec(memory_space=pltpu.SMEM)
    return pl.pallas_call(
        modulation_body,
        out_shape=jax.ShapeDtypeStruct((NY, 8, mod_weight.shape[-1]), F32),
        in_specs=[smem, vmem, vmem],
        out_specs=vmem,
        compiler_params=pltpu.CompilerParams(vmem_limit_bytes=8 * 2**20),
        name="modulation",
    )(facts, all_gaps, mod_weight)


def centre_body(x_ref, out_ref):
    rows, cols = x_ref.shape
    x = x_ref[...]
    mean = (jnp.sum(x, -1, keepdims=True) / cols).astype(BF).astype(F32)
    out_ref[:rows, :] = (x - mean).astype(BF)
    along = jnp.transpose(jnp.broadcast_to(mean, (rows, HD)))
    out_ref[rows : rows + EXTRA, :] = jnp.zeros((EXTRA, cols), BF)
    out_ref[rows : rows + EXTRA, :rows] = along[:EXTRA].astype(BF)


def centre(x):
    rows, cols = x.shape
    vmem = pl.BlockSpec(memory_space=pltpu.VMEM)
    return pl.pallas_call(
        centre_body,
        out_shape=jax.ShapeDtypeStruct((rows + EXTRA, cols), BF),
        in_specs=[vmem],
        out_specs=vmem,
        compiler_params=pltpu.CompilerParams(vmem_limit_bytes=8 * 2**20),
        name="centre",
    )(x)


def block_body(first, tok, cols, facts, *refs):
    states, refs = refs[:4], refs[4:]
    if not first:
        incs, refs = refs[:4], refs[4:]
    mods, qkv_hbm, out_hbm, refs = refs[0], refs[1], refs[2], refs[3:]
    tots, ins, (wv, wo, nrm, qkv, att, sems) = refs[:4], refs[4:8], refs[8:]
    width = NY * cols
    depth = width // CUTS
    copies = [
        pltpu.make_async_copy(qkv_hbm.at[p, pl.ds(c * depth, depth)], wv.at[p, pl.ds(c * depth, depth)], sems.at[p * CUTS + c])
        for p in range(3)
        for c in range(CUTS)
    ]
    copies.append(pltpu.make_async_copy(out_hbm, wo, sems.at[3 * CUTS]))
    for copy in copies:
        copy.start()
    me = facts[1]
    n_rows = 2 * tok if first else tok
    centres = [jnp.transpose(states[k][n_rows:, :n_rows].astype(F32))[:, 0:1] for k in range(NY)]
    for s in range(2):
        rows = pl.ds(s * tok, tok)
        parts = []
        for k in range(NY):
            if first:
                x = states[k][rows, :].astype(F32) + centres[k][s * tok : (s + 1) * tok]
            else:
                x = states[k][:tok, :].astype(F32) + centres[k]
                if s == 1:
                    x = x + incs[k][...].astype(F32)
            parts.append(x)
        mean = sum(jnp.sum(x, -1, keepdims=True) for x in parts) / width
        var = sum(jnp.sum((x - mean) * (x - mean), -1, keepdims=True) for x in parts) / width
        inv = lax.rsqrt(var + 1e-06)
        for k in range(NY):
            src = lax.rem(me + NY - k, NY)
            shift = mods[src, 3 * s : 3 * s + 1, :]
            scale = mods[src, 3 * s + 1 : 3 * s + 2, :]
            normed = (parts[k] - mean) * inv * (1.0 + scale) + shift
            at = pl.multiple_of(src * cols, cols)
            nrm[rows, pl.ds(at, cols)] = normed.astype(BF)
    for p in range(3):
        for copy in copies[p * CUTS : (p + 1) * CUTS]:
            copy.wait()
        qkv[p] = jnp.dot(nrm[...], wv[p], preferred_element_type=F32).astype(BF)
    cells = [(pl.ds(s * tok, tok), pl.ds(h * HD, HD)) for s in range(2) for h in range(cols // HD)]
    scores = [
        lax.dot_general(
            qkv[0, rows, lanes], qkv[1, rows, lanes], (((1,), (1,)), ((), ())), preferred_element_type=F32
        )
        * (1.0 / math.sqrt(HD))
        for rows, lanes in cells
    ]
    weights = [jnp.exp(x - jnp.max(x, -1, keepdims=True)) for x in scores]
    probs = [(w * (1.0 / jnp.sum(w, -1, keepdims=True))).astype(BF) for w in weights]
    for (rows, lanes), prob in zip(cells, probs, strict=True):
        att[rows, lanes] = jnp.dot(prob, qkv[2, rows, lanes], preferred_element_type=F32).astype(BF)
    copies[-1].wait()
    neg = [-(facts[3 + s].astype(F32) / LEVELS) for s in range(2)]
    for k in (1, 2, 3, 0):
        dst = lax.rem(me + k, NY)
        at = pl.multiple_of(dst * cols, cols)
        made = jnp.dot(att[...], wo[:, pl.ds(at, cols)], preferred_element_type=F32)
        inc0 = made[:tok] * (mods[dst, 2:3, :] * neg[0])
        inc1 = made[tok:] * (mods[dst, 5:6, :] * neg[1])
        tots[k][...] = (inc0 + inc1).astype(tots[k].dtype)
        ins[k][...] = inc0.astype(ins[k].dtype)


def block(first, facts, states, mods, qkv_weight, out_weight):
    cols, width = out_weight.shape
    tok = (states[0].shape[0] - EXTRA) // (2 if first else 1)

    def body(*refs):
        block_body(first, tok, cols, *refs)

    vmem = pl.BlockSpec(memory_space=pltpu.VMEM)
    smem = pl.BlockSpec(memory_space=pltpu.SMEM)
    hbm = pl.BlockSpec(memory_space=pltpu.HBM)
    outs = [jax.ShapeDtypeStruct((tok, cols), F32 if k == 0 else BF) for k in range(NY)]
    made = pl.pallas_call(
        body,
        out_shape=outs + outs,
        in_specs=[smem] + [vmem] * (len(states) + 1) + [hbm, hbm],
        out_specs=[vmem] * (2 * NY),
        scratch_shapes=[
            pltpu.VMEM(qkv_weight.shape, BF),
            pltpu.VMEM(out_weight.shape, BF),
            pltpu.VMEM((2 * tok, width), BF),
            pltpu.VMEM((3, 2 * tok, cols), BF),
            pltpu.VMEM((2 * tok, cols), BF),
            pltpu.SemaphoreType.DMA((3 * CUTS + 1,)),
        ],
        compiler_params=pltpu.CompilerParams(vmem_limit_bytes=LIMIT * 2**20),
        cost_estimate=pl.CostEstimate(
            flops=2 * 2 * tok * width * 4 * cols, bytes_accessed=8 * width * cols, transcendentals=0
        ),
        name="block",
    )(facts, *states, mods, qkv_weight, out_weight)
    return made[:NY], made[NY:]


def body(trajectory, offset, step_gaps, qkv_weight, out_weight, mod_weight):
    steps_here, tok, cols = trajectory.shape
    tm, tp = lax.axis_index("tm"), lax.axis_index("tp")
    x_at, z_at, core = tm // (NZ * NC), (tm // NC) % NZ, tm % NC
    half = tok // 2

    sent = jnp.broadcast_to(step_gaps[None, None], (NX * NZ * NC, 1, steps_here))
    trajectory, sent = lax.optimization_barrier((trajectory, sent))
    all_gaps = lax.all_to_all(sent, "tm", 0, 0)
    states = spread(centre(trajectory.reshape(steps_here * tok, cols)))
    place_of = jnp.arange(8, dtype=jnp.int32)
    facts = jnp.where(place_of == 0, tm, jnp.where(place_of == 1, tp, jnp.where(place_of == 2, offset[0], 0)))
    facts = jnp.where(place_of == 3, step_gaps[0], jnp.where(place_of == 4, step_gaps[1], facts))
    weights = (jnp.transpose(qkv_weight, (1, 0, 2)), out_weight)
    made = modulation(facts, all_gaps, jnp.transpose(mod_weight, (1, 0, 2)))
    mods = lax.all_to_all(made, "tp", 0, 0)

    def deliver(own, shares):
        total = own
        for k in (1, 2, 3):
            total = total + lax.ppermute(shares[k], "tp", ring(k)).astype(F32)
        return total

    def before_me(sent, beside_z, beside_x):
        kind = sent.dtype
        other = lax.ppermute(sent, "tm", SWAP)
        chip = sent.astype(F32) + other.astype(F32)
        mine = jnp.where(core == 0, chip[:half], chip[half:]).astype(kind)
        plane = mine.astype(F32)
        below = jnp.zeros_like(plane)
        for k in (1, 2, 3):
            came = lax.ppermute(mine, "tm", z_shift(k)).astype(F32)
            plane = plane + came
            below = below + jnp.where(z_at >= k, came, 0.0)
        plane, beside_z = lax.optimization_barrier((plane.astype(kind), beside_z))
        made = beside_x(beside_z)
        for k in (1, 2, 3):
            came = lax.ppermute(plane, "tm", x_shift(k)).astype(F32)
            below = below + jnp.where(x_at >= k, came, 0.0)
        below, made = lax.optimization_barrier((below.astype(kind), made))
        rest = lax.ppermute(below, "tm", SWAP)
        low = jnp.where(core == 0, below, rest)
        high = jnp.where(core == 0, rest, below)
        prefix = jnp.concatenate([low, high], 0).astype(F32)
        return prefix, other.astype(F32), beside_z, made

    start = jnp.where(tm == 0, trajectory[0], 0.0)
    tots, ins = block(True, facts, states, mods, *weights)
    total = deliver(tots[0], tots)
    total, ins = lax.optimization_barrier((total, ins))
    prefix, other, _, incs = before_me(total + start, deliver(ins[0], ins), lambda inc: spread(inc.astype(BF)))
    entry = prefix + jnp.where(core == 0, start, other)
    tots, ins = block(False, facts, spread(centre(entry)) + incs, mods, *weights)
    total_2 = deliver(tots[0], tots)
    total_2, ins = lax.optimization_barrier((total_2, ins))
    prefix, other, inc0, _ = before_me((total_2 - total).astype(BF), deliver(ins[0], ins), lambda inc: ())
    entry = entry + prefix + jnp.where(core == 0, 0.0, other)
    return jnp.stack([entry + inc0, entry + total_2])


def solution(mesh):
    placed = (
        P("tm", None, "tp"),
        P(),
        P("tm"),
        P(None, None, "tp"),
        P("tp", None),
        P(None, None, "tp"),
    )
    return jax.shard_map(
        body, mesh=mesh, in_specs=placed, out_specs=P("tm", None, "tp"), check_vma=False
    )
```

```python
import math

import jax
import jax.numpy as jnp
from jax import lax
from jax.experimental import pallas as pl
from jax.experimental.pallas import tpu as pltpu
from jax.sharding import PartitionSpec as P

HD = 128
FREQ = 256
EXTRA = 8
LIMIT = 48
ROOM = 28
LEVELS = 320
NX, NZ, NC, NY = 4, 4, 2, 4
BF = jnp.bfloat16
F32 = jnp.float32


def ring(k):
    return [(i, (i + k) % NY) for i in range(NY)]


def place(x, z, c):
    return (x * NZ + z) * NC + c


CHIPS = [(x, z, c) for x in range(NX) for z in range(NZ) for c in range(NC)]
SWAP = [(place(x, z, c), place(x, z, 1 - c)) for x, z, c in CHIPS]


def z_shift(k):
    return [(place(x, z, c), place(x, (z + k) % NZ, c)) for x, z, c in CHIPS]


def x_shift(k):
    return [(place(x, z, c), place((x + k) % NX, z, c)) for x, z, c in CHIPS]


def spread(array):
    return [array] + [lax.ppermute(array, "tp", ring(k)) for k in (1, 2, 3)]


def modulation_body(facts, all_gaps, mod_ref, out_ref):
    half_freq = FREQ // 2
    gaps = all_gaps[...]
    earlier = lax.broadcasted_iota(jnp.int32, gaps.shape, 0) < facts[0]
    before = jnp.sum(jnp.where(earlier, gaps, 0), 0)
    level = before[:, 0:1] + before[:, 1:2] + facts[2]
    lane = lax.broadcasted_iota(jnp.int32, (1, half_freq), 1).astype(F32)
    frequencies = jnp.exp(-math.log(10000.0) * lane / half_freq)
    rows = []
    for here in (level, level + facts[3]):
        angles = 1000.0 * (1.0 - here.astype(F32) / LEVELS) * frequencies
        rows.append(jnp.concatenate([jnp.cos(angles), jnp.sin(angles)], -1))
    index = lax.broadcasted_iota(jnp.int32, (8, FREQ), 0)
    embed_rows = jnp.where(index == 0, rows[0], jnp.where(index == 1, rows[1], 0.0)).astype(BF)
    out_ref[...] = jnp.zeros_like(out_ref)
    for p in range(3):
        made = jnp.dot(embed_rows, mod_ref[p], preferred_element_type=F32)
        for s in range(2):
            for y in range(NY):
                out_ref[y, 3 * s + p : 3 * s + p + 1, :] = made[s : s + 1]


def modulation(facts, all_gaps, mod_weight):
    vmem = pl.BlockSpec(memory_space=pltpu.VMEM)
    smem = pl.BlockSpec(memory_space=pltpu.SMEM)
    return pl.pallas_call(
        modulation_body,
        out_shape=jax.ShapeDtypeStruct((NY, 8, mod_weight.shape[-1]), F32),
        in_specs=[smem, vmem, vmem],
        out_specs=vmem,
        compiler_params=pltpu.CompilerParams(vmem_limit_bytes=8 * 2**20),
        name="modulation",
    )(facts, all_gaps, mod_weight)


def centre_body(x_ref, out_ref):
    rows, cols = x_ref.shape
    x = x_ref[...]
    mean = (jnp.sum(x, -1, keepdims=True) / cols).astype(BF).astype(F32)
    out_ref[:rows, :] = (x - mean).astype(BF)
    along = jnp.transpose(jnp.broadcast_to(mean, (rows, HD)))
    out_ref[rows : rows + EXTRA, :] = jnp.zeros((EXTRA, cols), BF)
    out_ref[rows : rows + EXTRA, :rows] = along[:EXTRA].astype(BF)


def centre(x):
    rows, cols = x.shape
    vmem = pl.BlockSpec(memory_space=pltpu.VMEM)
    return pl.pallas_call(
        centre_body,
        out_shape=jax.ShapeDtypeStruct((rows + EXTRA, cols), BF),
        in_specs=[vmem],
        out_specs=vmem,
        compiler_params=pltpu.CompilerParams(vmem_limit_bytes=8 * 2**20),
        name="centre",
    )(x)


def attend(rows_of, tok, cols, nrm, wv, qkv, att, ready):
    for p in range(3):
        ready(p)
        qkv[p] = jnp.dot(nrm[...], wv[p], preferred_element_type=F32).astype(BF)
    cells = [(pl.ds(r * tok, tok), pl.ds(h * HD, HD)) for r in range(rows_of) for h in range(cols // HD)]
    scores = [
        lax.dot_general(
            qkv[0, rows, lanes], qkv[1, rows, lanes], (((1,), (1,)), ((), ())), preferred_element_type=F32
        )
        * (1.0 / math.sqrt(HD))
        for rows, lanes in cells
    ]
    weights = [jnp.exp(x - jnp.max(x, -1, keepdims=True)) for x in scores]
    probs = [(w * (1.0 / jnp.sum(w, -1, keepdims=True))).astype(BF) for w in weights]
    for (rows, lanes), prob in zip(cells, probs, strict=True):
        att[rows, lanes] = jnp.dot(prob, qkv[2, rows, lanes], preferred_element_type=F32).astype(BF)


def normalise(parts, s, row, tok, cols, me, mods, nrm):
    width = NY * cols
    mean = sum(jnp.sum(x, -1, keepdims=True) for x in parts) / width
    var = sum(jnp.sum((x - mean) * (x - mean), -1, keepdims=True) for x in parts) / width
    inv = lax.rsqrt(var + 1e-06)
    for k in range(NY):
        src = lax.rem(me + NY - k, NY)
        shift = mods[src, 3 * s : 3 * s + 1, :]
        scale = mods[src, 3 * s + 1 : 3 * s + 2, :]
        normed = (parts[k] - mean) * inv * (1.0 + scale) + shift
        nrm[row : row + tok, pl.ds(pl.multiple_of(src * cols, cols), cols)] = normed.astype(BF)
    return mean


def both_body(tok, cols, facts, *refs):
    states, mods, qkv_hbm, out_hbm = refs[:4], refs[4], refs[5], refs[6]
    tots, ins, (start_ref, nrm, qkv, att, wv, wo, sems) = refs[7:11], refs[11:15], refs[15:]
    copies = [pltpu.make_async_copy(qkv_hbm.at[p], wv.at[p], sems.at[p]) for p in range(3)]
    copies.append(pltpu.make_async_copy(out_hbm, wo, sems.at[3]))
    for copy in copies:
        copy.start()
    me = facts[1]
    centres = [jnp.transpose(states[k][2 * tok :, : 2 * tok].astype(F32))[:, 0:1] for k in range(NY)]
    for s in range(2):
        rows = pl.ds(s * tok, tok)
        parts = [states[k][rows, :].astype(F32) + centres[k][s * tok : (s + 1) * tok] for k in range(NY)]
        mean = normalise(parts, s, s * tok, tok, cols, me, mods, nrm)
        if s == 0:
            start_ref[...] = parts[0] - mean
    attend(2, tok, cols, nrm, wv, qkv, att, lambda p: copies[p].wait())
    copies[3].wait()
    neg = [-(facts[3 + s].astype(F32) / LEVELS) for s in range(2)]
    for k in (1, 2, 3, 0):
        dst = lax.rem(me + k, NY)
        at = pl.multiple_of(dst * cols, cols)
        made = jnp.dot(att[...], wo[:, pl.ds(at, cols)], preferred_element_type=F32)
        inc0 = made[:tok] * (mods[dst, 2:3, :] * neg[0])
        inc1 = made[tok:] * (mods[dst, 5:6, :] * neg[1])
        tots[k][...] = (inc0 + inc1).astype(tots[k].dtype)
        ins[k][...] = inc0.astype(ins[k].dtype)


def one_body(s, tok, cols, facts, *refs):
    states, mods, wv, wo, refs = refs[:4], refs[4], refs[5], refs[6], refs[7:]
    if s == 1:
        earlier, refs = refs[0], refs[1:]
    else:
        kept, refs = refs[0], refs[1:]
    shares, (nrm, qkv, att) = refs[:4], refs[4:]
    me = facts[1]
    normalise([states[k][...].astype(F32) for k in range(NY)], s, 0, tok, cols, me, mods, nrm)
    attend(1, tok, cols, nrm, wv, qkv, att, lambda p: None)
    neg = -(facts[3 + s].astype(F32) / LEVELS)
    for k in (1, 2, 3, 0):
        dst = lax.rem(me + k, NY)
        at = pl.multiple_of(dst * cols, cols)
        made = jnp.dot(att[...], wo[:, pl.ds(at, cols)], preferred_element_type=F32)
        made = made * (mods[dst, 3 * s + 2 : 3 * s + 3, :] * neg)
        if s == 1:
            made = made + earlier[k]
        else:
            kept[k] = made
        shares[k][...] = made.astype(shares[k].dtype)


def specs():
    return (pl.BlockSpec(memory_space=m) for m in (pltpu.VMEM, pltpu.SMEM, pltpu.HBM))


def share_shapes(tok, cols):
    return [jax.ShapeDtypeStruct((tok, cols), F32 if k == 0 else BF) for k in range(NY)]


def rows_scratch(rows, cols):
    return [pltpu.VMEM((rows, NY * cols), BF), pltpu.VMEM((3, rows, cols), BF), pltpu.VMEM((rows, cols), BF)]


def estimate(steps, tok, cols):
    return pl.CostEstimate(
        flops=2 * steps * tok * NY * cols * 4 * cols, bytes_accessed=8 * NY * cols * cols, transcendentals=0
    )


def both(facts, states, mods, qkv_weight, out_weight):
    cols, _ = out_weight.shape
    tok = (states[0].shape[0] - EXTRA) // 2
    vmem, smem, hbm = specs()
    shares = share_shapes(tok, cols)
    made = pl.pallas_call(
        lambda *refs: both_body(tok, cols, *refs),
        out_shape=shares + shares + shares[:1],
        in_specs=[smem] + [vmem] * 5 + [hbm, hbm],
        out_specs=[vmem] * 9,
        scratch_shapes=rows_scratch(2 * tok, cols)
        + [pltpu.VMEM(qkv_weight.shape, BF), pltpu.VMEM(out_weight.shape, BF), pltpu.SemaphoreType.DMA((4,))],
        compiler_params=pltpu.CompilerParams(vmem_limit_bytes=LIMIT * 2**20),
        cost_estimate=estimate(2, tok, cols),
        name="both",
    )(facts, *states, mods, qkv_weight, out_weight)
    return made[:NY], made[NY : 2 * NY], made[2 * NY]


def one(s, facts, states, mods, weights, earlier):
    tok, cols = states[0].shape
    vmem, smem, _ = specs()
    kept = [jax.ShapeDtypeStruct((NY, tok, cols), F32)] * (s == 0)
    return pl.pallas_call(
        lambda *refs: one_body(s, tok, cols, *refs),
        out_shape=kept + share_shapes(tok, cols),
        in_specs=[smem] + [vmem] * (7 + len(earlier)),
        out_specs=[vmem] * (len(kept) + NY),
        scratch_shapes=rows_scratch(tok, cols),
        compiler_params=pltpu.CompilerParams(vmem_limit_bytes=ROOM * 2**20),
        cost_estimate=estimate(1, tok, cols),
        name="one",
    )(facts, *states, mods, *weights, *earlier)


def arrive_body(facts, after, wv, wo, out):
    for i in range(8):
        out[i] = facts[i]


def arrive(facts, after, qkv_weight, out_weight):
    vmem, smem, hbm = specs()
    return pl.pallas_call(
        arrive_body,
        out_shape=jax.ShapeDtypeStruct(facts.shape, facts.dtype),
        in_specs=[smem, hbm, vmem, vmem],
        out_specs=smem,
        compiler_params=pltpu.CompilerParams(vmem_limit_bytes=ROOM * 2**20),
        name="arrive",
    )(facts, after, qkv_weight, out_weight)


def body(trajectory, offset, step_gaps, qkv_weight, out_weight, mod_weight):
    steps_here, tok, cols = trajectory.shape
    tm, tp = lax.axis_index("tm"), lax.axis_index("tp")
    x_at, z_at, core = tm // (NZ * NC), (tm // NC) % NZ, tm % NC
    half = tok // 2

    sent = jnp.broadcast_to(step_gaps[None, None], (NX * NZ * NC, 1, steps_here))
    trajectory, sent = lax.optimization_barrier((trajectory, sent))
    all_gaps = lax.all_to_all(sent, "tm", 0, 0)
    states = spread(centre(trajectory.reshape(steps_here * tok, cols)))
    place_of = jnp.arange(8, dtype=jnp.int32)
    facts = jnp.where(place_of == 0, tm, jnp.where(place_of == 1, tp, jnp.where(place_of == 2, offset[0], 0)))
    facts = jnp.where(place_of == 3, step_gaps[0], jnp.where(place_of == 4, step_gaps[1], facts))
    weights = (jnp.transpose(qkv_weight, (1, 0, 2)), out_weight)
    made = modulation(facts, all_gaps, jnp.transpose(mod_weight, (1, 0, 2)))
    mods = lax.all_to_all(made, "tp", 0, 0)

    def deliver(own, shares):
        total = own
        for k in (1, 2, 3):
            total = total + lax.ppermute(shares[k], "tp", ring(k)).astype(F32)
        return total

    def before_me(own, sent, beside_z):
        now = []

        def send(value, pairs):
            mine, theirs = sent[len(now)] if sent else ((0.0), (0.0,) * len(pairs))
            message = (value - mine).astype(BF)
            came = [lax.ppermute(message, "tm", p).astype(F32) + t for p, t in zip(pairs, theirs, strict=True)]
            now.append((message.astype(F32) + mine, came))
            return came

        (other,) = send(own, [SWAP])
        chip = own + other
        mine = jnp.where(core == 0, chip[:half], chip[half:])
        came = send(mine, [z_shift(k) for k in (1, 2, 3)])
        plane = mine + came[0] + came[1] + came[2]
        below = sum(jnp.where(z_at >= k, c, 0.0) for k, c in zip((1, 2, 3), came, strict=True))
        plane, beside_z = lax.optimization_barrier((plane, beside_z))
        came = send(plane, [x_shift(k) for k in (1, 2, 3)])
        below = below + sum(jnp.where(x_at >= k, c, 0.0) for k, c in zip((1, 2, 3), came, strict=True))
        (rest,) = send(below, [SWAP])
        low = jnp.where(core == 0, below, rest)
        high = jnp.where(core == 0, rest, below)
        return jnp.concatenate([low, high], 0), other, now, beside_z

    tots, ins, start = both(facts, states, mods, *weights)
    start = jnp.where(tm == 0, start, 0.0)
    total = deliver(tots[0], tots)
    total, ins = lax.optimization_barrier((total, ins))
    prefix, other, sent, inc0 = before_me(total + start, (), deliver(ins[0], ins))
    entry = prefix + jnp.where(core == 0, start, other)
    first, second = spread(entry.astype(BF)), spread((entry + inc0).astype(BF))
    facts = arrive(facts, first[0], *weights)
    kept, *ins = one(0, facts, first, mods, weights, [])
    inc0 = deliver(ins[0], ins)
    tots = one(1, facts, second, mods, weights, [kept])
    start = jnp.where(tm == 0, trajectory[0], 0.0)
    total, inc0 = lax.optimization_barrier((deliver(tots[0], tots), inc0))
    prefix, other, _, _ = before_me(total + start, sent, ())
    entry = prefix + jnp.where(core == 0, start, other)
    return jnp.stack([entry + inc0, entry + total])


def solution(mesh):
    placed = (
        P("tm", None, "tp"),
        P(),
        P("tm"),
        P(None, None, "tp"),
        P("tp", None),
        P(None, None, "tp"),
    )
    return jax.shard_map(
        body, mesh=mesh, in_specs=placed, out_specs=P("tm", None, "tp"), check_vma=False
    )
```

```python
import math

import jax
import jax.numpy as jnp
from jax import lax
from jax.experimental import pallas as pl
from jax.experimental.pallas import tpu as pltpu
from jax.sharding import PartitionSpec as P

HD = 128
FREQ = 256
EXTRA = 8
LIMIT = 30
ROOM = 28
WAIT = 10**10
LEVELS = 320
NX, NZ, NC, NY = 4, 4, 2, 4
BF = jnp.bfloat16
F32 = jnp.float32


def ring(k):
    return [(i, (i + k) % NY) for i in range(NY)]


def place(x, z, c):
    return (x * NZ + z) * NC + c


CHIPS = [(x, z, c) for x in range(NX) for z in range(NZ) for c in range(NC)]
SWAP = [(place(x, z, c), place(x, z, 1 - c)) for x, z, c in CHIPS]


def z_shift(k):
    return [(place(x, z, c), place(x, (z + k) % NZ, c)) for x, z, c in CHIPS]


def x_shift(k):
    return [(place(x, z, c), place((x + k) % NX, z, c)) for x, z, c in CHIPS]


def spread(array):
    return [array] + [lax.ppermute(array, "tp", ring(k)) for k in (1, 2, 3)]


def modulation_body(facts, all_gaps, mod_ref, out_ref):
    half_freq = FREQ // 2
    gaps = all_gaps[...]
    earlier = lax.broadcasted_iota(jnp.int32, gaps.shape, 0) < facts[0]
    before = jnp.sum(jnp.where(earlier, gaps, 0), 0)
    level = before[:, 0:1] + before[:, 1:2] + facts[2]
    lane = lax.broadcasted_iota(jnp.int32, (1, half_freq), 1).astype(F32)
    frequencies = jnp.exp(-math.log(10000.0) * lane / half_freq)
    rows = []
    for here in (level, level + facts[3]):
        angles = 1000.0 * (1.0 - here.astype(F32) / LEVELS) * frequencies
        rows.append(jnp.concatenate([jnp.cos(angles), jnp.sin(angles)], -1))
    index = lax.broadcasted_iota(jnp.int32, (8, FREQ), 0)
    embed_rows = jnp.where(index == 0, rows[0], jnp.where(index == 1, rows[1], 0.0)).astype(BF)
    out_ref[...] = jnp.zeros_like(out_ref)
    for p in range(3):
        made = jnp.dot(embed_rows, mod_ref[p], preferred_element_type=F32)
        for s in range(2):
            for y in range(NY):
                out_ref[y, 3 * s + p : 3 * s + p + 1, :] = made[s : s + 1]


def modulation(facts, all_gaps, mod_weight):
    vmem = pl.BlockSpec(memory_space=pltpu.VMEM)
    smem = pl.BlockSpec(memory_space=pltpu.SMEM)
    return pl.pallas_call(
        modulation_body,
        out_shape=jax.ShapeDtypeStruct((NY, 8, mod_weight.shape[-1]), F32),
        in_specs=[smem, vmem, vmem],
        out_specs=vmem,
        compiler_params=pltpu.CompilerParams(vmem_limit_bytes=8 * 2**20),
        cost_estimate=pl.CostEstimate(flops=WAIT, bytes_accessed=10**6, transcendentals=0),
        name="modulation",
    )(facts, all_gaps, mod_weight)


def centre_body(x_ref, out_ref):
    rows, cols = x_ref.shape
    x = x_ref[...]
    mean = (jnp.sum(x, -1, keepdims=True) / cols).astype(BF).astype(F32)
    out_ref[:rows, :] = (x - mean).astype(BF)
    along = jnp.transpose(jnp.broadcast_to(mean, (rows, HD)))
    out_ref[rows : rows + EXTRA, :] = jnp.zeros((EXTRA, cols), BF)
    out_ref[rows : rows + EXTRA, :rows] = along[:EXTRA].astype(BF)


def centre(x):
    rows, cols = x.shape
    vmem = pl.BlockSpec(memory_space=pltpu.VMEM)
    return pl.pallas_call(
        centre_body,
        out_shape=jax.ShapeDtypeStruct((rows + EXTRA, cols), BF),
        in_specs=[vmem],
        out_specs=vmem,
        compiler_params=pltpu.CompilerParams(vmem_limit_bytes=8 * 2**20),
        name="centre",
    )(x)


def attend(rows_of, tok, cols, nrm, wv, qkv, att, ready):
    for p in range(3):
        ready(p)
        qkv[p] = jnp.dot(nrm[...], wv[p], preferred_element_type=F32).astype(BF)
    cells = [(pl.ds(r * tok, tok), pl.ds(h * HD, HD)) for r in range(rows_of) for h in range(cols // HD)]
    scores = [
        lax.dot_general(
            qkv[0, rows, lanes], qkv[1, rows, lanes], (((1,), (1,)), ((), ())), preferred_element_type=F32
        )
        * (1.0 / math.sqrt(HD))
        for rows, lanes in cells
    ]
    weights = [jnp.exp(x - jnp.max(x, -1, keepdims=True)) for x in scores]
    probs = [(w * (1.0 / jnp.sum(w, -1, keepdims=True))).astype(BF) for w in weights]
    for (rows, lanes), prob in zip(cells, probs, strict=True):
        att[rows, lanes] = jnp.dot(prob, qkv[2, rows, lanes], preferred_element_type=F32).astype(BF)


def normalise(parts, s, row, tok, cols, me, mods, nrm):
    width = NY * cols
    mean = sum(jnp.sum(x, -1, keepdims=True) for x in parts) / width
    var = sum(jnp.sum((x - mean) * (x - mean), -1, keepdims=True) for x in parts) / width
    inv = lax.rsqrt(var + 1e-06)
    for k in range(NY):
        src = lax.rem(me + NY - k, NY)
        shift = mods[src, 3 * s : 3 * s + 1, :]
        scale = mods[src, 3 * s + 1 : 3 * s + 2, :]
        normed = (parts[k] - mean) * inv * (1.0 + scale) + shift
        nrm[row : row + tok, pl.ds(pl.multiple_of(src * cols, cols), cols)] = normed.astype(BF)
    return mean


def both_body(tok, cols, facts, *refs):
    states, mods, wv, wo = refs[:4], refs[4], refs[5], refs[6]
    tots, ins, (start_ref, nrm, qkv, att) = refs[7:11], refs[11:15], refs[15:]
    me = facts[1]
    centres = [jnp.transpose(states[k][2 * tok :, : 2 * tok].astype(F32))[:, 0:1] for k in range(NY)]
    for s in range(2):
        rows = pl.ds(s * tok, tok)
        parts = [states[k][rows, :].astype(F32) + centres[k][s * tok : (s + 1) * tok] for k in range(NY)]
        mean = normalise(parts, s, s * tok, tok, cols, me, mods, nrm)
        if s == 0:
            start_ref[...] = parts[0] - mean
    attend(2, tok, cols, nrm, wv, qkv, att, lambda p: None)
    neg = [-(facts[3 + s].astype(F32) / LEVELS) for s in range(2)]
    for k in (1, 2, 3, 0):
        dst = lax.rem(me + k, NY)
        at = pl.multiple_of(dst * cols, cols)
        made = jnp.dot(att[...], wo[:, pl.ds(at, cols)], preferred_element_type=F32)
        inc0 = made[:tok] * (mods[dst, 2:3, :] * neg[0])
        inc1 = made[tok:] * (mods[dst, 5:6, :] * neg[1])
        tots[k][...] = (inc0 + inc1).astype(tots[k].dtype)
        ins[k][...] = inc0.astype(ins[k].dtype)


def one_body(s, tok, cols, facts, *refs):
    states, mods, wv, wo, refs = refs[:4], refs[4], refs[5], refs[6], refs[7:]
    if s == 1:
        earlier, refs = refs[0], refs[1:]
    else:
        kept, refs = refs[0], refs[1:]
    shares, (nrm, qkv, att) = refs[:4], refs[4:]
    me = facts[1]
    normalise([states[k][...].astype(F32) for k in range(NY)], s, 0, tok, cols, me, mods, nrm)
    attend(1, tok, cols, nrm, wv, qkv, att, lambda p: None)
    neg = -(facts[3 + s].astype(F32) / LEVELS)
    for k in (1, 2, 3, 0):
        dst = lax.rem(me + k, NY)
        at = pl.multiple_of(dst * cols, cols)
        made = jnp.dot(att[...], wo[:, pl.ds(at, cols)], preferred_element_type=F32)
        made = made * (mods[dst, 3 * s + 2 : 3 * s + 3, :] * neg)
        if s == 1:
            made = made + earlier[k]
        else:
            kept[k] = made
        shares[k][...] = made.astype(shares[k].dtype)


def specs():
    return (pl.BlockSpec(memory_space=m) for m in (pltpu.VMEM, pltpu.SMEM, pltpu.HBM))


def share_shapes(tok, cols):
    return [jax.ShapeDtypeStruct((tok, cols), F32 if k == 0 else BF) for k in range(NY)]


def rows_scratch(rows, cols):
    return [pltpu.VMEM((rows, NY * cols), BF), pltpu.VMEM((3, rows, cols), BF), pltpu.VMEM((rows, cols), BF)]


def estimate(steps, tok, cols):
    return pl.CostEstimate(
        flops=2 * steps * tok * NY * cols * 4 * cols, bytes_accessed=8 * NY * cols * cols, transcendentals=0
    )


def both(facts, states, mods, qkv_weight, out_weight):
    cols, _ = out_weight.shape
    tok = (states[0].shape[0] - EXTRA) // 2
    vmem, smem, _ = specs()
    shares = share_shapes(tok, cols)
    made = pl.pallas_call(
        lambda *refs: both_body(tok, cols, *refs),
        out_shape=shares + shares + shares[:1],
        in_specs=[smem] + [vmem] * 7,
        out_specs=[vmem] * 9,
        scratch_shapes=rows_scratch(2 * tok, cols),
        compiler_params=pltpu.CompilerParams(vmem_limit_bytes=LIMIT * 2**20),
        cost_estimate=estimate(2, tok, cols),
        name="both",
    )(facts, *states, mods, qkv_weight, out_weight)
    return made[:NY], made[NY : 2 * NY], made[2 * NY]


def one(s, facts, states, mods, weights, earlier):
    tok, cols = states[0].shape
    vmem, smem, _ = specs()
    kept = [jax.ShapeDtypeStruct((NY, tok, cols), F32)] * (s == 0)
    return pl.pallas_call(
        lambda *refs: one_body(s, tok, cols, *refs),
        out_shape=kept + share_shapes(tok, cols),
        in_specs=[smem] + [vmem] * (7 + len(earlier)),
        out_specs=[vmem] * (len(kept) + NY),
        scratch_shapes=rows_scratch(tok, cols),
        compiler_params=pltpu.CompilerParams(vmem_limit_bytes=ROOM * 2**20),
        cost_estimate=estimate(1, tok, cols),
        name="one",
    )(facts, *states, mods, *weights, *earlier)


def arrive_body(facts, after, out):
    for i in range(8):
        out[i] = facts[i]


def arrive(facts, after):
    _, smem, hbm = specs()
    return pl.pallas_call(
        arrive_body,
        out_shape=jax.ShapeDtypeStruct(facts.shape, facts.dtype),
        in_specs=[smem, hbm],
        out_specs=smem,
        compiler_params=pltpu.CompilerParams(vmem_limit_bytes=2**20),
        cost_estimate=pl.CostEstimate(flops=WAIT, bytes_accessed=1024, transcendentals=0),
        name="arrive",
    )(facts, after)


def body(trajectory, offset, step_gaps, qkv_weight, out_weight, mod_weight):
    steps_here, tok, cols = trajectory.shape
    tm, tp = lax.axis_index("tm"), lax.axis_index("tp")
    x_at, z_at, core = tm // (NZ * NC), (tm // NC) % NZ, tm % NC
    half = tok // 2

    sent = jnp.broadcast_to(step_gaps[None, None], (NX * NZ * NC, 1, steps_here))
    trajectory, sent = lax.optimization_barrier((trajectory, sent))
    all_gaps = lax.all_to_all(sent, "tm", 0, 0)
    states = spread(centre(trajectory.reshape(steps_here * tok, cols)))
    place_of = jnp.arange(8, dtype=jnp.int32)
    facts = jnp.where(place_of == 0, tm, jnp.where(place_of == 1, tp, jnp.where(place_of == 2, offset[0], 0)))
    facts = jnp.where(place_of == 3, step_gaps[0], jnp.where(place_of == 4, step_gaps[1], facts))
    weights = (jnp.transpose(qkv_weight, (1, 0, 2)), out_weight)
    made = modulation(facts, all_gaps, jnp.transpose(mod_weight, (1, 0, 2)))
    mods = lax.all_to_all(made, "tp", 0, 0)

    def deliver(own, shares):
        total = own
        for k in (1, 2, 3):
            total = total + lax.ppermute(shares[k], "tp", ring(k)).astype(F32)
        return total

    def before_me(own, sent, beside_z):
        now = []

        def send(value, pairs):
            mine, theirs = sent[len(now)] if sent else ((0.0), (0.0,) * len(pairs))
            message = (value - mine).astype(BF)
            came = [lax.ppermute(message, "tm", p).astype(F32) + t for p, t in zip(pairs, theirs, strict=True)]
            now.append((message.astype(F32) + mine, came))
            return came

        (other,) = send(own, [SWAP])
        chip = own + other
        mine = jnp.where(core == 0, chip[:half], chip[half:])
        came = send(mine, [z_shift(k) for k in (1, 2, 3)])
        plane = mine + came[0] + came[1] + came[2]
        below = sum(jnp.where(z_at >= k, c, 0.0) for k, c in zip((1, 2, 3), came, strict=True))
        plane, beside_z = lax.optimization_barrier((plane, beside_z))
        came = send(plane, [x_shift(k) for k in (1, 2, 3)])
        below = below + sum(jnp.where(x_at >= k, c, 0.0) for k, c in zip((1, 2, 3), came, strict=True))
        (rest,) = send(below, [SWAP])
        low = jnp.where(core == 0, below, rest)
        high = jnp.where(core == 0, rest, below)
        return jnp.concatenate([low, high], 0), other, now, beside_z

    tots, ins, start = both(facts, states, mods, *weights)
    start = jnp.where(tm == 0, start, 0.0)
    total = deliver(tots[0], tots)
    total, ins = lax.optimization_barrier((total, ins))
    prefix, other, sent, inc0 = before_me(total + start, (), deliver(ins[0], ins))
    entry = prefix + jnp.where(core == 0, start, other)
    first, second = spread(entry.astype(BF)), spread((entry + inc0).astype(BF))
    facts = arrive(facts, first[0])
    kept, *ins = one(0, facts, first, mods, weights, [])
    inc0 = deliver(ins[0], ins)
    tots = one(1, facts, second, mods, weights, [kept])
    start = jnp.where(tm == 0, trajectory[0], 0.0)
    total, inc0 = lax.optimization_barrier((deliver(tots[0], tots), inc0))
    prefix, other, _, _ = before_me(total + start, sent, ())
    entry = prefix + jnp.where(core == 0, start, other)
    return jnp.stack([entry + inc0, entry + total])


def solution(mesh):
    placed = (
        P("tm", None, "tp"),
        P(),
        P("tm"),
        P(None, None, "tp"),
        P("tp", None),
        P(None, None, "tp"),
    )
    return jax.shard_map(
        body, mesh=mesh, in_specs=placed, out_specs=P("tm", None, "tp"), check_vma=False
    )
```

```python
import math

import jax
import jax.numpy as jnp
from jax import lax
from jax.experimental import pallas as pl
from jax.experimental.pallas import tpu as pltpu
from jax.sharding import PartitionSpec as P

HD = 128
FREQ = 256
EXTRA = 8
LIMIT = 30
ROOM = 28
WAIT = 10**10
LEVELS = 320
NX, NZ, NC, NY = 4, 4, 2, 4
BF = jnp.bfloat16
F32 = jnp.float32


def ring(k):
    return [(i, (i + k) % NY) for i in range(NY)]


def place(x, z, c):
    return (x * NZ + z) * NC + c


CHIPS = [(x, z, c) for x in range(NX) for z in range(NZ) for c in range(NC)]
SWAP = [(place(x, z, c), place(x, z, 1 - c)) for x, z, c in CHIPS]


def z_shift(k):
    return [(place(x, z, c), place(x, (z + k) % NZ, c)) for x, z, c in CHIPS]


def x_shift(k):
    return [(place(x, z, c), place((x + k) % NX, z, c)) for x, z, c in CHIPS]


def spread(array):
    far = lax.ppermute(array, "tp", ring(2))
    return [array, lax.ppermute(array, "tp", ring(1)), far, lax.ppermute(array, "tp", ring(3))]


def modulation_body(facts, all_gaps, mod_ref, out_ref):
    half_freq = FREQ // 2
    gaps = all_gaps[...]
    earlier = lax.broadcasted_iota(jnp.int32, gaps.shape, 0) < facts[0]
    before = jnp.sum(jnp.where(earlier, gaps, 0), 0)
    level = before[:, 0:1] + before[:, 1:2] + facts[2]
    lane = lax.broadcasted_iota(jnp.int32, (1, half_freq), 1).astype(F32)
    frequencies = jnp.exp(-math.log(10000.0) * lane / half_freq)
    rows = []
    for here in (level, level + facts[3]):
        angles = 1000.0 * (1.0 - here.astype(F32) / LEVELS) * frequencies
        rows.append(jnp.concatenate([jnp.cos(angles), jnp.sin(angles)], -1))
    index = lax.broadcasted_iota(jnp.int32, (8, FREQ), 0)
    embed_rows = jnp.where(index == 0, rows[0], jnp.where(index == 1, rows[1], 0.0)).astype(BF)
    out_ref[...] = jnp.zeros_like(out_ref)
    for p in range(3):
        made = jnp.dot(embed_rows, mod_ref[p], preferred_element_type=F32)
        for s in range(2):
            for y in range(NY):
                out_ref[y, 3 * s + p : 3 * s + p + 1, :] = made[s : s + 1]


def modulation(facts, all_gaps, mod_weight):
    vmem = pl.BlockSpec(memory_space=pltpu.VMEM)
    smem = pl.BlockSpec(memory_space=pltpu.SMEM)
    return pl.pallas_call(
        modulation_body,
        out_shape=jax.ShapeDtypeStruct((NY, 8, mod_weight.shape[-1]), F32),
        in_specs=[smem, vmem, vmem],
        out_specs=vmem,
        compiler_params=pltpu.CompilerParams(vmem_limit_bytes=8 * 2**20),
        cost_estimate=pl.CostEstimate(flops=WAIT, bytes_accessed=10**6, transcendentals=0),
        name="modulation",
    )(facts, all_gaps, mod_weight)


def centre_body(x_ref, out_ref):
    rows, cols = x_ref.shape
    x = x_ref[...]
    mean = (jnp.sum(x, -1, keepdims=True) / cols).astype(BF).astype(F32)
    out_ref[:rows, :] = (x - mean).astype(BF)
    along = jnp.transpose(jnp.broadcast_to(mean, (rows, HD)))
    out_ref[rows : rows + EXTRA, :] = jnp.zeros((EXTRA, cols), BF)
    out_ref[rows : rows + EXTRA, :rows] = along[:EXTRA].astype(BF)


def centre(x):
    rows, cols = x.shape
    vmem = pl.BlockSpec(memory_space=pltpu.VMEM)
    return pl.pallas_call(
        centre_body,
        out_shape=jax.ShapeDtypeStruct((rows + EXTRA, cols), BF),
        in_specs=[vmem],
        out_specs=vmem,
        compiler_params=pltpu.CompilerParams(vmem_limit_bytes=8 * 2**20),
        name="centre",
    )(x)


def attend(rows_of, tok, cols, nrm, wv, qkv, att, ready):
    for p in range(3):
        ready(p)
        qkv[p] = jnp.dot(nrm[...], wv[p], preferred_element_type=F32).astype(BF)
    cells = [(pl.ds(r * tok, tok), pl.ds(h * HD, HD)) for r in range(rows_of) for h in range(cols // HD)]
    scores = [
        lax.dot_general(
            qkv[0, rows, lanes], qkv[1, rows, lanes], (((1,), (1,)), ((), ())), preferred_element_type=F32
        )
        * (1.0 / math.sqrt(HD))
        for rows, lanes in cells
    ]
    weights = [jnp.exp(x - jnp.max(x, -1, keepdims=True)) for x in scores]
    probs = [(w * (1.0 / jnp.sum(w, -1, keepdims=True))).astype(BF) for w in weights]
    for (rows, lanes), prob in zip(cells, probs, strict=True):
        att[rows, lanes] = jnp.dot(prob, qkv[2, rows, lanes], preferred_element_type=F32).astype(BF)


def normalise(parts, s, row, tok, cols, me, mods, nrm):
    width = NY * cols
    mean = sum(jnp.sum(x, -1, keepdims=True) for x in parts) / width
    var = sum(jnp.sum((x - mean) * (x - mean), -1, keepdims=True) for x in parts) / width
    inv = lax.rsqrt(var + 1e-06)
    for k in range(NY):
        src = lax.rem(me + NY - k, NY)
        shift = mods[src, 3 * s : 3 * s + 1, :]
        scale = mods[src, 3 * s + 1 : 3 * s + 2, :]
        normed = (parts[k] - mean) * inv * (1.0 + scale) + shift
        nrm[row : row + tok, pl.ds(pl.multiple_of(src * cols, cols), cols)] = normed.astype(BF)
    return mean


def both_body(tok, cols, facts, *refs):
    states, mods, wv, wo = refs[:4], refs[4], refs[5], refs[6]
    tots, ins, (start_ref, nrm, qkv, att) = refs[7:11], refs[11:15], refs[15:]
    me = facts[1]
    centres = [jnp.transpose(states[k][2 * tok :, : 2 * tok].astype(F32))[:, 0:1] for k in range(NY)]
    for s in range(2):
        rows = pl.ds(s * tok, tok)
        parts = [states[k][rows, :].astype(F32) + centres[k][s * tok : (s + 1) * tok] for k in range(NY)]
        mean = normalise(parts, s, s * tok, tok, cols, me, mods, nrm)
        if s == 0:
            start_ref[...] = parts[0] - mean
    attend(2, tok, cols, nrm, wv, qkv, att, lambda p: None)
    neg = [-(facts[3 + s].astype(F32) / LEVELS) for s in range(2)]
    for k in (1, 2, 3, 0):
        dst = lax.rem(me + k, NY)
        at = pl.multiple_of(dst * cols, cols)
        made = jnp.dot(att[...], wo[:, pl.ds(at, cols)], preferred_element_type=F32)
        inc0 = made[:tok] * (mods[dst, 2:3, :] * neg[0])
        inc1 = made[tok:] * (mods[dst, 5:6, :] * neg[1])
        tots[k][...] = (inc0 + inc1).astype(tots[k].dtype)
        ins[k][...] = inc0.astype(ins[k].dtype)


def one_body(s, tok, cols, facts, *refs):
    states, mods, wv, wo, refs = refs[:4], refs[4], refs[5], refs[6], refs[7:]
    if s == 1:
        earlier, refs = refs[0], refs[1:]
    else:
        kept, refs = refs[0], refs[1:]
    shares, (nrm, qkv, att) = refs[:4], refs[4:]
    me = facts[1]
    normalise([states[k][...].astype(F32) for k in range(NY)], s, 0, tok, cols, me, mods, nrm)
    attend(1, tok, cols, nrm, wv, qkv, att, lambda p: None)
    neg = -(facts[3 + s].astype(F32) / LEVELS)
    for k in (1, 2, 3, 0):
        dst = lax.rem(me + k, NY)
        at = pl.multiple_of(dst * cols, cols)
        made = jnp.dot(att[...], wo[:, pl.ds(at, cols)], preferred_element_type=F32)
        made = made * (mods[dst, 3 * s + 2 : 3 * s + 3, :] * neg)
        if s == 1:
            made = made + earlier[k]
        else:
            kept[k] = made
        shares[k][...] = made.astype(shares[k].dtype)


def specs():
    return (pl.BlockSpec(memory_space=m) for m in (pltpu.VMEM, pltpu.SMEM, pltpu.HBM))


def share_shapes(tok, cols):
    return [jax.ShapeDtypeStruct((tok, cols), F32 if k == 0 else BF) for k in range(NY)]


def rows_scratch(rows, cols):
    return [pltpu.VMEM((rows, NY * cols), BF), pltpu.VMEM((3, rows, cols), BF), pltpu.VMEM((rows, cols), BF)]


def estimate(steps, tok, cols):
    return pl.CostEstimate(
        flops=2 * steps * tok * NY * cols * 4 * cols, bytes_accessed=8 * NY * cols * cols, transcendentals=0
    )


def both(facts, states, mods, qkv_weight, out_weight):
    cols, _ = out_weight.shape
    tok = (states[0].shape[0] - EXTRA) // 2
    vmem, smem, _ = specs()
    shares = share_shapes(tok, cols)
    made = pl.pallas_call(
        lambda *refs: both_body(tok, cols, *refs),
        out_shape=shares + shares + shares[:1],
        in_specs=[smem] + [vmem] * 7,
        out_specs=[vmem] * 9,
        scratch_shapes=rows_scratch(2 * tok, cols),
        compiler_params=pltpu.CompilerParams(vmem_limit_bytes=LIMIT * 2**20),
        cost_estimate=estimate(2, tok, cols),
        name="both",
    )(facts, *states, mods, qkv_weight, out_weight)
    return made[:NY], made[NY : 2 * NY], made[2 * NY]


def one(s, facts, states, mods, weights, earlier):
    tok, cols = states[0].shape
    vmem, smem, _ = specs()
    kept = [jax.ShapeDtypeStruct((NY, tok, cols), F32)] * (s == 0)
    return pl.pallas_call(
        lambda *refs: one_body(s, tok, cols, *refs),
        out_shape=kept + share_shapes(tok, cols),
        in_specs=[smem] + [vmem] * (7 + len(earlier)),
        out_specs=[vmem] * (len(kept) + NY),
        scratch_shapes=rows_scratch(tok, cols),
        compiler_params=pltpu.CompilerParams(vmem_limit_bytes=ROOM * 2**20),
        cost_estimate=estimate(1, tok, cols),
        name="one",
    )(facts, *states, mods, *weights, *earlier)


def arrive_body(facts, after, out):
    for i in range(8):
        out[i] = facts[i]


def arrive(facts, after):
    _, smem, hbm = specs()
    return pl.pallas_call(
        arrive_body,
        out_shape=jax.ShapeDtypeStruct(facts.shape, facts.dtype),
        in_specs=[smem, hbm],
        out_specs=smem,
        compiler_params=pltpu.CompilerParams(vmem_limit_bytes=2**20),
        cost_estimate=pl.CostEstimate(flops=WAIT, bytes_accessed=1024, transcendentals=0),
        name="arrive",
    )(facts, after)


def body(trajectory, offset, step_gaps, qkv_weight, out_weight, mod_weight):
    steps_here, tok, cols = trajectory.shape
    tm, tp = lax.axis_index("tm"), lax.axis_index("tp")
    x_at, z_at, core = tm // (NZ * NC), (tm // NC) % NZ, tm % NC
    half = tok // 2

    sent = jnp.broadcast_to(step_gaps[None, None], (NX * NZ * NC, 1, steps_here))
    trajectory, sent = lax.optimization_barrier((trajectory, sent))
    all_gaps = lax.all_to_all(sent, "tm", 0, 0)
    states = spread(centre(trajectory.reshape(steps_here * tok, cols)))
    place_of = jnp.arange(8, dtype=jnp.int32)
    facts = jnp.where(place_of == 0, tm, jnp.where(place_of == 1, tp, jnp.where(place_of == 2, offset[0], 0)))
    facts = jnp.where(place_of == 3, step_gaps[0], jnp.where(place_of == 4, step_gaps[1], facts))
    weights = (jnp.transpose(qkv_weight, (1, 0, 2)), out_weight)
    made = modulation(facts, all_gaps, jnp.transpose(mod_weight, (1, 0, 2)))
    mods = lax.all_to_all(made, "tp", 0, 0)

    def deliver(own, shares):
        total = own
        for k in (2, 1, 3):
            total = total + lax.ppermute(shares[k], "tp", ring(k)).astype(F32)
        return total

    def before_me(own, sent, beside_z):
        now = []

        def send(value, pairs):
            mine, theirs = sent[len(now)] if sent else ((0.0), (0.0,) * len(pairs))
            message = (value - mine).astype(BF)
            came = [lax.ppermute(message, "tm", p).astype(F32) + t for p, t in zip(pairs, theirs, strict=True)]
            now.append((message.astype(F32) + mine, came))
            return came

        (other,) = send(own, [SWAP])
        chip = own + other
        mine = jnp.where(core == 0, chip[:half], chip[half:])
        came = send(mine, [z_shift(k) for k in (1, 2, 3)])
        plane = mine + came[0] + came[1] + came[2]
        below = sum(jnp.where(z_at >= k, c, 0.0) for k, c in zip((1, 2, 3), came, strict=True))
        plane, beside_z = lax.optimization_barrier((plane, beside_z))
        came = send(plane, [x_shift(k) for k in (1, 2, 3)])
        below = below + sum(jnp.where(x_at >= k, c, 0.0) for k, c in zip((1, 2, 3), came, strict=True))
        (rest,) = send(below, [SWAP])
        low = jnp.where(core == 0, below, rest)
        high = jnp.where(core == 0, rest, below)
        return jnp.concatenate([low, high], 0), other, now, beside_z

    tots, ins, start = both(facts, states, mods, *weights)
    start = jnp.where(tm == 0, start, 0.0)
    total = deliver(tots[0], tots)
    total, ins = lax.optimization_barrier((total, ins))
    prefix, other, sent, inc0 = before_me(total + start, (), deliver(ins[0], ins))
    entry = prefix + jnp.where(core == 0, start, other)
    first, second = spread(entry.astype(BF)), spread((entry + inc0).astype(BF))
    facts = arrive(facts, first[0])
    kept, *ins = one(0, facts, first, mods, weights, [])
    inc0 = deliver(ins[0], ins)
    tots = one(1, facts, second, mods, weights, [kept])
    start = jnp.where(tm == 0, trajectory[0], 0.0)
    total, inc0 = lax.optimization_barrier((deliver(tots[0], tots), inc0))
    prefix, other, _, _ = before_me(total + start, sent, ())
    entry = prefix + jnp.where(core == 0, start, other)
    return jnp.stack([entry + inc0, entry + total])


def solution(mesh):
    placed = (
        P("tm", None, "tp"),
        P(),
        P("tm"),
        P(None, None, "tp"),
        P("tp", None),
        P(None, None, "tp"),
    )
    return jax.shard_map(
        body, mesh=mesh, in_specs=placed, out_specs=P("tm", None, "tp"), check_vma=False
    )
```

```python
import math

import jax
import jax.numpy as jnp
from jax import lax
from jax.experimental import pallas as pl
from jax.experimental.pallas import tpu as pltpu
from jax.sharding import PartitionSpec as P

HD = 128
FREQ = 256
EXTRA = 8
LIMIT = 30
ROOM = 28
WAIT = 10**10
LEVELS = 320
NX, NZ, NC, NY = 4, 4, 2, 4
BF = jnp.bfloat16
F32 = jnp.float32


def ring(k):
    return [(i, (i + k) % NY) for i in range(NY)]


def place(x, z, c):
    return (x * NZ + z) * NC + c


CHIPS = [(x, z, c) for x in range(NX) for z in range(NZ) for c in range(NC)]
SWAP = [(place(x, z, c), place(x, z, 1 - c)) for x, z, c in CHIPS]


def z_shift(k):
    return [(place(x, z, c), place(x, (z + k) % NZ, c)) for x, z, c in CHIPS]


def x_shift(k):
    return [(place(x, z, c), place((x + k) % NX, z, c)) for x, z, c in CHIPS]


def spread(array):
    far = lax.ppermute(array, "tp", ring(2))
    return [array, lax.ppermute(array, "tp", ring(1)), far, lax.ppermute(array, "tp", ring(3))]


def modulation_body(facts, all_gaps, mod_ref, out_ref):
    half_freq = FREQ // 2
    gaps = all_gaps[...]
    earlier = lax.broadcasted_iota(jnp.int32, gaps.shape, 0) < facts[0]
    before = jnp.sum(jnp.where(earlier, gaps, 0), 0)
    level = before[:, 0:1] + before[:, 1:2] + facts[2]
    lane = lax.broadcasted_iota(jnp.int32, (1, half_freq), 1).astype(F32)
    frequencies = jnp.exp(-math.log(10000.0) * lane / half_freq)
    rows = []
    for here in (level, level + facts[3]):
        angles = 1000.0 * (1.0 - here.astype(F32) / LEVELS) * frequencies
        rows.append(jnp.concatenate([jnp.cos(angles), jnp.sin(angles)], -1))
    index = lax.broadcasted_iota(jnp.int32, (8, FREQ), 0)
    embed_rows = jnp.where(index == 0, rows[0], jnp.where(index == 1, rows[1], 0.0)).astype(BF)
    out_ref[...] = jnp.zeros_like(out_ref)
    for p in range(3):
        made = jnp.dot(embed_rows, mod_ref[p], preferred_element_type=F32)
        for s in range(2):
            for y in range(NY):
                out_ref[y, 3 * s + p : 3 * s + p + 1, :] = made[s : s + 1]


def modulation(facts, all_gaps, mod_weight):
    vmem = pl.BlockSpec(memory_space=pltpu.VMEM)
    smem = pl.BlockSpec(memory_space=pltpu.SMEM)
    return pl.pallas_call(
        modulation_body,
        out_shape=jax.ShapeDtypeStruct((NY, 8, mod_weight.shape[-1]), F32),
        in_specs=[smem, vmem, vmem],
        out_specs=vmem,
        compiler_params=pltpu.CompilerParams(vmem_limit_bytes=8 * 2**20),
        cost_estimate=pl.CostEstimate(flops=WAIT, bytes_accessed=10**6, transcendentals=0),
        name="modulation",
    )(facts, all_gaps, mod_weight)


def centre_body(x_ref, out_ref):
    rows, cols = x_ref.shape
    x = x_ref[...]
    mean = (jnp.sum(x, -1, keepdims=True) / cols).astype(BF).astype(F32)
    out_ref[:rows, :] = (x - mean).astype(BF)
    along = jnp.transpose(jnp.broadcast_to(mean, (rows, HD)))
    out_ref[rows : rows + EXTRA, :] = jnp.zeros((EXTRA, cols), BF)
    out_ref[rows : rows + EXTRA, :rows] = along[:EXTRA].astype(BF)


def centre(x):
    rows, cols = x.shape
    vmem = pl.BlockSpec(memory_space=pltpu.VMEM)
    return pl.pallas_call(
        centre_body,
        out_shape=jax.ShapeDtypeStruct((rows + EXTRA, cols), BF),
        in_specs=[vmem],
        out_specs=vmem,
        compiler_params=pltpu.CompilerParams(vmem_limit_bytes=8 * 2**20),
        name="centre",
    )(x)


def attend(rows_of, tok, cols, nrm, wv, qkv, att, ready):
    for p in range(3):
        ready(p)
        qkv[p] = jnp.dot(nrm[...], wv[p], preferred_element_type=F32).astype(BF)
    cells = [(pl.ds(r * tok, tok), pl.ds(h * HD, HD)) for r in range(rows_of) for h in range(cols // HD)]
    scores = [
        lax.dot_general(
            qkv[0, rows, lanes], qkv[1, rows, lanes], (((1,), (1,)), ((), ())), preferred_element_type=F32
        )
        * (1.0 / math.sqrt(HD))
        for rows, lanes in cells
    ]
    weights = [jnp.exp(x - jnp.max(x, -1, keepdims=True)) for x in scores]
    probs = [(w * (1.0 / jnp.sum(w, -1, keepdims=True))).astype(BF) for w in weights]
    for (rows, lanes), prob in zip(cells, probs, strict=True):
        att[rows, lanes] = jnp.dot(prob, qkv[2, rows, lanes], preferred_element_type=F32).astype(BF)


def normalise(parts, s, row, tok, cols, me, mods, nrm):
    width = NY * cols
    mean = sum(jnp.sum(x, -1, keepdims=True) for x in parts) / width
    var = sum(jnp.sum((x - mean) * (x - mean), -1, keepdims=True) for x in parts) / width
    inv = lax.rsqrt(var + 1e-06)
    for k in range(NY):
        src = lax.rem(me + NY - k, NY)
        shift = mods[src, 3 * s : 3 * s + 1, :]
        scale = mods[src, 3 * s + 1 : 3 * s + 2, :]
        normed = (parts[k] - mean) * inv * (1.0 + scale) + shift
        nrm[row : row + tok, pl.ds(pl.multiple_of(src * cols, cols), cols)] = normed.astype(BF)
    return mean


def both_body(tok, cols, facts, *refs):
    states, mods, wv, wo = refs[:4], refs[4], refs[5], refs[6]
    tots, ins, (start_ref, nrm, qkv, att) = refs[7:11], refs[11:15], refs[15:]
    me = facts[1]
    centres = [jnp.transpose(states[k][2 * tok :, : 2 * tok].astype(F32))[:, 0:1] for k in range(NY)]
    for s in range(2):
        rows = pl.ds(s * tok, tok)
        parts = [states[k][rows, :].astype(F32) + centres[k][s * tok : (s + 1) * tok] for k in range(NY)]
        mean = normalise(parts, s, s * tok, tok, cols, me, mods, nrm)
        if s == 0:
            start_ref[...] = parts[0] - mean
    attend(2, tok, cols, nrm, wv, qkv, att, lambda p: None)
    neg = [-(facts[3 + s].astype(F32) / LEVELS) for s in range(2)]
    for k in (1, 2, 3, 0):
        dst = lax.rem(me + k, NY)
        at = pl.multiple_of(dst * cols, cols)
        made = jnp.dot(att[...], wo[:, pl.ds(at, cols)], preferred_element_type=F32)
        inc0 = made[:tok] * (mods[dst, 2:3, :] * neg[0])
        inc1 = made[tok:] * (mods[dst, 5:6, :] * neg[1])
        tots[k][...] = (inc0 + inc1).astype(tots[k].dtype)
        ins[k][...] = inc0.astype(ins[k].dtype)


def one_body(s, tok, cols, facts, *refs):
    states, mods, wv, wo, refs = refs[:4], refs[4], refs[5], refs[6], refs[7:]
    if s == 1:
        earlier, refs = refs[0], refs[1:]
    else:
        kept, refs = refs[0], refs[1:]
    shares, (nrm, qkv, att) = refs[:4], refs[4:]
    me = facts[1]
    normalise([states[k][...].astype(F32) for k in range(NY)], s, 0, tok, cols, me, mods, nrm)
    attend(1, tok, cols, nrm, wv, qkv, att, lambda p: None)
    neg = -(facts[3 + s].astype(F32) / LEVELS)
    for k in (1, 2, 3, 0):
        dst = lax.rem(me + k, NY)
        at = pl.multiple_of(dst * cols, cols)
        made = jnp.dot(att[...], wo[:, pl.ds(at, cols)], preferred_element_type=F32)
        made = made * (mods[dst, 3 * s + 2 : 3 * s + 3, :] * neg)
        if s == 1:
            made = made + earlier[k]
        else:
            kept[k] = made
        shares[k][...] = made.astype(shares[k].dtype)


def specs():
    return (pl.BlockSpec(memory_space=m) for m in (pltpu.VMEM, pltpu.SMEM, pltpu.HBM))


def share_shapes(tok, cols):
    return [jax.ShapeDtypeStruct((tok, cols), F32 if k == 0 else BF) for k in range(NY)]


def rows_scratch(rows, cols):
    return [pltpu.VMEM((rows, NY * cols), BF), pltpu.VMEM((3, rows, cols), BF), pltpu.VMEM((rows, cols), BF)]


def estimate(steps, tok, cols):
    return pl.CostEstimate(
        flops=2 * steps * tok * NY * cols * 4 * cols, bytes_accessed=8 * NY * cols * cols, transcendentals=0
    )


def both(facts, states, mods, qkv_weight, out_weight):
    cols, _ = out_weight.shape
    tok = (states[0].shape[0] - EXTRA) // 2
    vmem, smem, _ = specs()
    shares = share_shapes(tok, cols)
    made = pl.pallas_call(
        lambda *refs: both_body(tok, cols, *refs),
        out_shape=shares + shares + shares[:1],
        in_specs=[smem] + [vmem] * 7,
        out_specs=[vmem] * 9,
        scratch_shapes=rows_scratch(2 * tok, cols),
        compiler_params=pltpu.CompilerParams(vmem_limit_bytes=LIMIT * 2**20),
        cost_estimate=estimate(2, tok, cols),
        name="both",
    )(facts, *states, mods, qkv_weight, out_weight)
    return made[:NY], made[NY : 2 * NY], made[2 * NY]


def one(s, facts, states, mods, weights, earlier):
    tok, cols = states[0].shape
    vmem, smem, _ = specs()
    kept = [jax.ShapeDtypeStruct((NY, tok, cols), F32)] * (s == 0)
    return pl.pallas_call(
        lambda *refs: one_body(s, tok, cols, *refs),
        out_shape=kept + share_shapes(tok, cols),
        in_specs=[smem] + [vmem] * (7 + len(earlier)),
        out_specs=[vmem] * (len(kept) + NY),
        scratch_shapes=rows_scratch(tok, cols),
        compiler_params=pltpu.CompilerParams(vmem_limit_bytes=ROOM * 2**20),
        cost_estimate=estimate(1, tok, cols),
        name="one",
    )(facts, *states, mods, *weights, *earlier)


def arrive_body(facts, after, out):
    for i in range(8):
        out[i] = facts[i]


def arrive(facts, after):
    _, smem, hbm = specs()
    return pl.pallas_call(
        arrive_body,
        out_shape=jax.ShapeDtypeStruct(facts.shape, facts.dtype),
        in_specs=[smem, hbm],
        out_specs=smem,
        compiler_params=pltpu.CompilerParams(vmem_limit_bytes=2**20),
        cost_estimate=pl.CostEstimate(flops=WAIT, bytes_accessed=1024, transcendentals=0),
        name="arrive",
    )(facts, after)


def body(trajectory, offset, step_gaps, qkv_weight, out_weight, mod_weight):
    steps_here, tok, cols = trajectory.shape
    tm, tp = lax.axis_index("tm"), lax.axis_index("tp")
    x_at, z_at, core = tm // (NZ * NC), (tm // NC) % NZ, tm % NC
    half = tok // 2

    sent = jnp.broadcast_to(step_gaps[None, None], (NX * NZ * NC, 1, steps_here))
    trajectory, sent = lax.optimization_barrier((trajectory, sent))
    all_gaps = lax.all_to_all(sent, "tm", 0, 0)
    states = spread(centre(trajectory.reshape(steps_here * tok, cols)))
    place_of = jnp.arange(8, dtype=jnp.int32)
    facts = jnp.where(place_of == 0, tm, jnp.where(place_of == 1, tp, jnp.where(place_of == 2, offset[0], 0)))
    facts = jnp.where(place_of == 3, step_gaps[0], jnp.where(place_of == 4, step_gaps[1], facts))
    weights = (jnp.transpose(qkv_weight, (1, 0, 2)), out_weight)
    made = modulation(facts, all_gaps, jnp.transpose(mod_weight, (1, 0, 2)))
    mods = lax.all_to_all(made, "tp", 0, 0)

    def deliver(own, shares):
        total = own
        for k in (2, 1, 3):
            total = total + lax.ppermute(shares[k], "tp", ring(k)).astype(F32)
        return total

    def before_me(own, sent, beside_z):
        now = []

        def send(value, pairs):
            mine, theirs = sent[len(now)] if sent else ((0.0), (0.0,) * len(pairs))
            message = (value - mine).astype(BF)
            came = [lax.ppermute(message, "tm", p).astype(F32) + t for p, t in zip(pairs, theirs, strict=True)]
            now.append((message.astype(F32) + mine, came))
            return came

        (other,) = send(own, [SWAP])
        chip = own + other
        mine = jnp.where(core == 0, chip[:half], chip[half:])
        came = send(mine, [z_shift(k) for k in (1, 2, 3)])
        plane = mine + came[1] + came[0] + came[2]
        below = sum(jnp.where(z_at >= k, c, 0.0) for k, c in zip((1, 2, 3), came, strict=True))
        plane, beside_z = lax.optimization_barrier((plane, beside_z))
        came = send(plane, [x_shift(k) for k in (1, 2, 3)])
        below = below + sum(jnp.where(x_at >= k, c, 0.0) for k, c in zip((1, 2, 3), came, strict=True))
        (rest,) = send(below, [SWAP])
        low = jnp.where(core == 0, below, rest)
        high = jnp.where(core == 0, rest, below)
        return jnp.concatenate([low, high], 0), other, now, beside_z

    tots, ins, start = both(facts, states, mods, *weights)
    start = jnp.where(tm == 0, start, 0.0)
    total = deliver(tots[0], tots)
    total, ins = lax.optimization_barrier((total, ins))
    prefix, other, sent, inc0 = before_me(total + start, (), deliver(ins[0], ins))
    entry = prefix + jnp.where(core == 0, start, other)
    first, second = spread(entry.astype(BF)), spread((entry + inc0).astype(BF))
    facts = arrive(facts, first[0])
    kept, *ins = one(0, facts, first, mods, weights, [])
    inc0 = deliver(ins[0], ins)
    tots = one(1, facts, second, mods, weights, [kept])
    start = jnp.where(tm == 0, trajectory[0], 0.0)
    total, inc0 = lax.optimization_barrier((deliver(tots[0], tots), inc0))
    prefix, other, _, _ = before_me(total + start, sent, ())
    entry = prefix + jnp.where(core == 0, start, other)
    return jnp.stack([entry + inc0, entry + total])


def solution(mesh):
    placed = (
        P("tm", None, "tp"),
        P(),
        P("tm"),
        P(None, None, "tp"),
        P("tp", None),
        P(None, None, "tp"),
    )
    return jax.shard_map(
        body, mesh=mesh, in_specs=placed, out_specs=P("tm", None, "tp"), check_vma=False
    )
```
